32 devices in a mesh: seq: 8 (over y, x, core), fsdp: 4 (over z).
Axes of the slice: x: 2, y: 2, z: 4, core: 2. Of those that a mesh axis runs over, the one named last changes fastest.
Arguments:
- tokens: bfloat16 [4, 16, 128, 1024], P('fsdp', 'seq'), may hold values from -6 to 6
- span_ids: int32 [4, 16], P('fsdp'), may hold values from 0 to 15, as said below
- attn_gain: float32 [1024], replicated, may hold values from 0.1 to 1.9
- w_query: bfloat16 [1024, 1024], P(('seq', 'fsdp')), may hold values from -0.1875 to 0.1875
- w_key: bfloat16 [1024, 512], P(('seq', 'fsdp')), may hold values from -0.1875 to 0.1875
- w_value: bfloat16 [1024, 512], P(('seq', 'fsdp')), may hold values from -0.1875 to 0.1875
- query_gain: float32 [64], replicated, may hold values from 0.1 to 1.9
- key_gain: float32 [64], replicated, may hold values from 0.1 to 1.9
- w_out: bfloat16 [1024, 1024], P(('seq', 'fsdp')), may hold values from -1.5 to 1.5
- ffn_gain: float32 [1024], replicated, may hold values from 0.1 to 1.9
- w_gate: bfloat16 [1024, 4608], P(('seq', 'fsdp')), may hold values from -0.1875 to 0.1875
- w_up: bfloat16 [1024, 4608], P(('seq', 'fsdp')), may hold values from -0.1875 to 0.1875
- w_down: bfloat16 [4608, 1024], P(('seq', 'fsdp')), may hold values from -0.09375 to 0.09375
- cotangent: bfloat16 [4, 16, 128, 1024], P('fsdp', 'seq'), may hold values from -12 to 12
Outputs:
- outputs: bfloat16 [4, 16, 128, 1024], P('fsdp', 'seq')
- grad_tokens: float32 [4, 16, 128, 1024], P('fsdp', 'seq')
- grad_attn_gain: float32 [1024], replicated
- grad_w_query: float32 [1024, 1024], P(('seq', 'fsdp'))
- grad_w_key: float32 [1024, 512], P(('seq', 'fsdp'))
- grad_w_value: float32 [1024, 512], P(('seq', 'fsdp'))
- grad_query_gain: float32 [64], replicated
- grad_key_gain: float32 [64], replicated
- grad_w_out: float32 [1024, 1024], P(('seq', 'fsdp'))
- grad_ffn_gain: float32 [1024], replicated
- grad_w_gate: float32 [1024, 4608], P(('seq', 'fsdp'))
- grad_w_up: float32 [1024, 4608], P(('seq', 'fsdp'))
- grad_w_down: float32 [4608, 1024], P(('seq', 'fsdp'))
The draws below stay inside these ranges and needn't reach their ends.
Inputs may be any that keep to these rules, and one draw needn't show every extreme that they name: `span_ids`: each row is a permutation of the 16 blocks of one sequence; slots 2i and 2i+1 hold blocks c and 15 - c.
All inputs are finite; a program needn't handle non-finite values.
Results may differ from the reference program's by a relative error of at most 0.018.
Values may be sent and summed in bfloat16 or wider, within the bound.
No kernel may reach another device: no remote copies, remote signals or barrier semaphores. Data moves between devices by JAX's collectives and lax.ppermute only.
A program may use at most 192 MiB of HBM per device.

```python
import math
import jax
import jax.numpy as jnp
from jax import lax

D = 1024
FF = 4608
HEADS = 16
KV_HEADS = 8
HEAD_DIM = 64
SPAN = 128
SPANS = 16
SEQ_LEN = 2048
SEQS = 4


def draw_span_ids(key, part):
    pair_count = SPANS // 2
    keys = jax.random.split(key, SEQS)

    def one_sequence(seq_key):
        key_order, key_flip = jax.random.split(seq_key)
        lower_half = jax.random.permutation(key_order, pair_count)
        flipped = jax.random.randint(key_flip, (pair_count,), 0, 2)
        leading = jnp.where(flipped == 1, SPANS - 1 - lower_half, lower_half)
        trailing = SPANS - 1 - leading
        return jnp.stack([leading, trailing], axis=1).reshape(SPANS).astype(jnp.int32)
    return jax.vmap(one_sequence)(keys)


def draw_cotangent(key, part):
    key_base = jax.random.fold_in(key, 0)
    seq_index = jnp.arange(SEQS, dtype=jnp.float32)[:, None, None, None]
    slot_index = jnp.arange(SPANS, dtype=jnp.float32)[None, :, None, None]
    rising = 1.0 + 2.0 * (seq_index * SPANS + slot_index) / max(SEQS * SPANS - 1, 1)
    base = jnp.clip(jax.random.normal(key_base, (SEQS, SPANS, SPAN, D), jnp.float32), -4.0, 4.0)
    return jnp.clip(base * rising, -12.0, 12.0).astype(jnp.bfloat16)


def block_scale(rng, dims, pieces, least, high):
    level = 1.0
    for dim, shards_of in pieces:
        heights = jax.random.uniform(jax.random.fold_in(jax.random.fold_in(rng, 6), dim), (shards_of,), jnp.float32, least / len(pieces), high / len(pieces))
        level = level * jnp.repeat(jnp.exp(heights), dims[dim] // shards_of).reshape((-1,) + (1,) * (len(dims) - 1 - dim))
    return level


def noise(key, shape, spread, most, cuts=(), kind=jnp.bfloat16):
    values = spread * jax.random.normal(key, shape, jnp.float32)
    if cuts:
        values = values * block_scale(key, shape, cuts, -0.22, 0.18)
    return jnp.clip(values, -most, most).astype(kind)


def setup_inputs(seed: int = 0) -> dict:
    key_of = jax.random.split(jax.random.key(seed), 15)
    tokens = noise(key_of[0], (SEQS, SPANS, SPAN, D), 1.0, 6.0, ((0, 4), (1, 8)))
    span_ids = draw_span_ids(jax.random.fold_in(key_of[14], 71), 0)
    attn_gain = jnp.clip(1.0 + 0.18 * jax.random.normal(key_of[2], (D,), jnp.float32), 0.1, 1.9)
    w_query = noise(key_of[3], (D, HEADS * HEAD_DIM), D ** -0.5, 0.1875, ((0, 32),))
    w_key = noise(key_of[4], (D, KV_HEADS * HEAD_DIM), D ** -0.5, 0.1875, ((0, 32),))
    w_value = noise(key_of[5], (D, KV_HEADS * HEAD_DIM), D ** -0.5, 0.1875, ((0, 32),))
    query_gain = jnp.clip(1.0 + 0.18 * jax.random.normal(key_of[6], (HEAD_DIM,), jnp.float32), 0.1, 1.9)
    key_gain = jnp.clip(1.0 + 0.18 * jax.random.normal(key_of[7], (HEAD_DIM,), jnp.float32), 0.1, 1.9)
    w_out = noise(key_of[8], (HEADS * HEAD_DIM, D), HEADS ** -0.5, 1.5, ((0, 32),))
    ffn_gain = jnp.clip(1.0 + 0.18 * jax.random.normal(key_of[9], (D,), jnp.float32), 0.1, 1.9)
    w_gate = noise(key_of[10], (D, FF), D ** -0.5, 0.1875, ((0, 32),))
    w_up = noise(key_of[11], (D, FF), D ** -0.5, 0.1875, ((0, 32),))
    w_down = noise(key_of[12], (FF, D), FF ** -0.5, 0.09375, ((0, 32),))
    cotangent = draw_cotangent(jax.random.fold_in(key_of[14], 71), 0)
    return dict(tokens=tokens, span_ids=span_ids, attn_gain=attn_gain, w_query=w_query, w_key=w_key, w_value=w_value, query_gain=query_gain, key_gain=key_gain, w_out=w_out, ffn_gain=ffn_gain, w_gate=w_gate, w_up=w_up, w_down=w_down, cotangent=cotangent)


EPSILON = 1e-06
THETA = 1000000.0
HIGHEST = lax.Precision.HIGHEST
NEGATIVE = -1e+30

@jax.custom_vjp
def low(v):
    return lax.optimization_barrier(v.astype(jnp.bfloat16)).astype(jnp.float32)

@jax.custom_vjp
def low_back(v):
    return v

def low_keep(v):
    return (low(v), None)

def low_pass(kept, grad):
    return (grad,)

def back_keep(v):
    return (v, None)

def back_low(kept, grad):
    return (low(grad),)
low.defvjp(low_keep, low_pass)
low_back.defvjp(back_keep, back_low)

def matmul(left, right):
    return jnp.dot(left, right, precision=HIGHEST, preferred_element_type=jnp.float32)

def rms_norm(values, gain):
    return values * lax.rsqrt(lax.optimization_barrier(jnp.mean(values * values, axis=-1, keepdims=True)) + EPSILON) * gain

def rope_angles(positions, head_width):
    half_width = head_width // 2
    indices = jnp.arange(half_width, dtype=jnp.float32)
    inverse = jnp.exp(indices * (-2.0 * math.log(THETA) / head_width))
    return positions.astype(jnp.float32)[:, None] * inverse[None, :]

def rotate(values, angles):
    half_width = values.shape[-1] // 2
    cosine = jnp.cos(angles)[:, None, :]
    sine = jnp.sin(angles)[:, None, :]
    front = values[..., :half_width]
    back = values[..., half_width:]
    return jnp.concatenate([front * cosine - back * sine, back * cosine + front * sine], axis=-1)

def attend(queries, keys, values, positions):
    length = queries.shape[0]
    block = min(512, length)
    scale = HEAD_DIM ** (-0.5)
    q_blocks = queries.reshape(length // block, block, KV_HEADS, HEADS // KV_HEADS, HEAD_DIM)
    p_blocks = positions.reshape(length // block, block)

    def one_block(item):
        q_part, pos_part = item
        scores = low_back(jnp.einsum('qgrd,kgd->grqk', q_part, keys, precision=HIGHEST) * scale)
        allowed = positions[None, None, None, :] <= pos_part[None, None, :, None]
        masked = jnp.where(allowed, scores, NEGATIVE)
        top = lax.optimization_barrier(jnp.max(masked, axis=-1, keepdims=True))
        total = lax.optimization_barrier(jnp.sum(jnp.where(allowed, jnp.exp(masked - top), 0.0), axis=-1, keepdims=True))
        log_total = top + jnp.log(total)
        probs = low(jnp.where(allowed, jnp.exp(masked - log_total), 0.0))
        return jnp.einsum('grqk,kgd->qgrd', probs, values, precision=HIGHEST)
    result = lax.map(jax.checkpoint(one_block), (q_blocks, p_blocks))
    return result.reshape(length, HEADS * HEAD_DIM)

def layer(inputs, positions, attn_gain, w_query, w_key, w_value, query_gain, key_gain, w_out, ffn_gain, w_gate, w_up, w_down):
    length = inputs.shape[0]
    angles = rope_angles(positions, HEAD_DIM)
    normed = low(rms_norm(inputs, attn_gain))
    q_raw = low_back(matmul(normed, w_query)).reshape(length, HEADS, HEAD_DIM)
    k_raw = low_back(matmul(normed, w_key)).reshape(length, KV_HEADS, HEAD_DIM)
    v_low = low(low_back(matmul(normed, w_value))).reshape(length, KV_HEADS, HEAD_DIM)
    q_low = low(rotate(rms_norm(q_raw, query_gain), angles))
    k_low = low(rotate(rms_norm(k_raw, key_gain), angles))
    attended = low(low_back(attend(q_low, k_low, v_low, positions)))
    branch = low_back(matmul(attended, w_out))
    middle = inputs + branch
    normed_two = low(rms_norm(middle, ffn_gain))
    gate = low_back(matmul(normed_two, w_gate))
    up_proj = low_back(matmul(normed_two, w_up))
    hidden = low(jax.nn.silu(gate) * up_proj)
    return middle + low_back(matmul(hidden, w_down))

def reference(tokens, span_ids, attn_gain, w_query, w_key, w_value, query_gain, key_gain, w_out, ffn_gain, w_gate, w_up, w_down, cotangent):
    params = tuple((weight.astype(jnp.float32) for weight in (attn_gain, w_query, w_key, w_value, query_gain, key_gain, w_out, ffn_gain, w_gate, w_up, w_down)))
    zeros = tuple((jnp.zeros(weight.shape, jnp.float32) for weight in params))

    def per_sequence(totals, item):
        seq_tokens, seq_ids, seq_cot = item
        positions = (seq_ids[:, None] * SPAN + jnp.arange(SPAN, dtype=jnp.int32)[None, :]).reshape(-1).astype(jnp.int32)
        inputs = seq_tokens.reshape(SEQ_LEN, D).astype(jnp.float32)

        def forward(values, *weights):
            return layer(values, positions, *weights)
        result, pull = jax.vjp(forward, inputs, *params)
        grads = pull(seq_cot.reshape(SEQ_LEN, D).astype(jnp.float32))
        totals = tuple((a + b for a, b in zip(totals, grads[1:])))
        return (totals, (result.astype(jnp.bfloat16).reshape(SPANS, SPAN, D), grads[0].reshape(SPANS, SPAN, D)))
    totals, (outputs, grad_tokens) = lax.scan(per_sequence, zeros, (tokens, span_ids, cotangent))
    return (outputs, grad_tokens, totals[0], totals[1], totals[2], totals[3], totals[4], totals[5], totals[6], totals[7], totals[8], totals[9], totals[10])
```

```python
import functools
import math

import jax
import jax.numpy as jnp
from jax import lax
from jax.experimental import pallas as pl
from jax.experimental.pallas import tpu as pltpu
from jax.sharding import PartitionSpec as P

EPSILON = 1e-06
THETA = 1000000.0
LOW = jnp.bfloat16
WIDE = jnp.float32
TILE = 256


def rope_tables(length, head_width):
    half_width = head_width // 2
    indices = jnp.arange(half_width, dtype=WIDE)
    inverse = jnp.exp(indices * (-2.0 * math.log(THETA) / head_width))
    angles = jnp.arange(length, dtype=jnp.int32).astype(WIDE)[:, None] * inverse[None, :]
    cosine = jnp.cos(angles)
    sine = jnp.sin(angles)
    return (
        jnp.concatenate([cosine, cosine], axis=-1),
        jnp.concatenate([-sine, sine], axis=-1),
    )


def rms_parts(values):
    inverse = lax.rsqrt(jnp.mean(values * values, axis=-1, keepdims=True) + EPSILON)
    return (values * inverse, inverse)


def norm_back(grad_out, normed, inverse, gain):
    scaled = grad_out * gain
    return inverse * (scaled - normed * jnp.mean(scaled * normed, axis=-1, keepdims=True))


def swap_halves(values):
    half = values.shape[-1] // 2
    return jnp.concatenate([values[:, half:], values[:, :half]], axis=-1)


def dot(left, right, dims=((1,), (0,))):
    return lax.dot_general(left, right, (dims, ((), ())), preferred_element_type=WIDE)


def forward_body(
    order, raw, query_gain, key_gain, cosine, sine,
    attended, queries, keys, values, outs, totals, acc,
    *, heads, width, span, length,
):
    spans = length // span
    per_tile = TILE // span
    tiles = length // TILE
    scale = width ** (-0.5)
    lane = lax.broadcasted_iota(jnp.int32, (span, width), 1)

    def prepare(place, _):
        slot = pl.multiple_of(order[place] * span, span)
        at = pl.multiple_of(place * span, span)
        part = raw[pl.ds(slot, span), :]
        cos_part = cosine[pl.ds(at, span), :]
        sin_part = sine[pl.ds(at, span), :]
        tile = place // per_tile
        inner = (place % per_tile) * span
        for head in range(heads + 1):
            normed, _ = rms_parts(part[:, head * width : (head + 1) * width])
            gained = normed * (query_gain[...] if head < heads else key_gain[...])
            turned = gained * cos_part + swap_halves(gained) * sin_part
            if head < heads:
                row = pl.multiple_of(head * TILE + inner, span)
                queries[tile, pl.ds(row, span), :] = (turned.astype(LOW).astype(WIDE) * scale).astype(LOW)
            else:
                keys[pl.ds(at, span), :] = turned.astype(LOW)
        value = part[:, (heads + 1) * width :].astype(LOW)
        values[pl.ds(at, span), :] = jnp.concatenate(
            [value, jnp.where(lane == 0, 1.0, 0.0).astype(LOW)], axis=-1
        )
        return 0

    lax.fori_loop(0, spans, prepare, 0)
    row_ids = lax.broadcasted_iota(jnp.int32, (heads * TILE, TILE), 0) % TILE
    col_ids = lax.broadcasted_iota(jnp.int32, (heads * TILE, TILE), 1)
    allowed = col_ids <= row_ids

    def one_tile(tile, _):
        query = queries[tile]

        def weights(step):
            at = pl.multiple_of(step * TILE, TILE)
            return jnp.exp(dot(query, keys[pl.ds(at, TILE), :], ((1,), (1,)))), at

        weight, at = weights(tile)
        weight = jnp.where(allowed, weight, 0.0).astype(LOW)
        acc[...] = dot(weight, values[pl.ds(at, TILE), :])

        def before(step, _):
            weight, at = weights(step)
            acc[...] += dot(weight.astype(LOW), values[pl.ds(at, TILE), :])
            return 0

        lax.fori_loop(0, tile, before, 0)
        total = acc[...]
        out = total[:, :width] / total[:, width : width + 1]
        outs[tile] = out
        turned = jnp.transpose(total)
        totals[tile] = jnp.broadcast_to(jnp.log(turned[width : width + 1, :]), (8, heads * TILE))
        low = out.astype(LOW)
        for part in range(per_tile):
            slot = pl.multiple_of(order[tile * per_tile + part] * span, span)
            pieces = [
                low[head * TILE + part * span : head * TILE + (part + 1) * span, :]
                for head in range(heads)
            ]
            attended[pl.ds(slot, span), :] = jnp.concatenate(pieces, axis=-1)
        return 0

    lax.fori_loop(0, tiles, one_tile, 0)


def attention_forward(order, raw, query_gain, key_gain, cosine, sine, heads, width, span):
    length = raw.shape[0]
    tiles = length // TILE
    vmem = pl.BlockSpec(memory_space=pltpu.VMEM)
    return pl.pallas_call(
        functools.partial(forward_body, heads=heads, width=width, span=span, length=length),
        name="attention_forward",
        in_specs=[pl.BlockSpec(memory_space=pltpu.SMEM)] + [vmem] * 5,
        out_specs=[vmem] * 6,
        out_shape=[
            jax.ShapeDtypeStruct((length, heads * width), LOW),
            jax.ShapeDtypeStruct((tiles, heads * TILE, width), LOW),
            jax.ShapeDtypeStruct((length, width), LOW),
            jax.ShapeDtypeStruct((length, 2 * width), LOW),
            jax.ShapeDtypeStruct((tiles, heads * TILE, width), WIDE),
            jax.ShapeDtypeStruct((tiles, 8, heads * TILE), WIDE),
        ],
        scratch_shapes=[pltpu.VMEM((heads * TILE, 2 * width), WIDE)],
        compiler_params=pltpu.CompilerParams(vmem_limit_bytes=48 * 1024 * 1024),
    )(order, raw, query_gain, key_gain, cosine, sine)


def backward_body(
    order, raw, grad_att, queries, keys, values, outs, totals,
    query_gain, key_gain, cosine, sine,
    grad_raw, gain_sums,
    grad_outs, grad_queries, grad_keys, grad_values, grad_turned, delta,
    *, heads, width, span, length,
):
    spans = length // span
    per_tile = TILE // span
    tiles = length // TILE
    scale = width ** (-0.5)
    key_ids = lax.broadcasted_iota(jnp.int32, (TILE, heads * TILE), 0)
    query_ids = lax.broadcasted_iota(jnp.int32, (TILE, heads * TILE), 1) % TILE
    allowed = key_ids <= query_ids

    def place_grads(place, _):
        slot = pl.multiple_of(order[place] * span, span)
        part = grad_att[pl.ds(slot, span), :]
        for head in range(heads):
            row = pl.multiple_of(head * TILE + (place % per_tile) * span, span)
            grad_outs[place // per_tile, pl.ds(row, span), :] = part[
                :, head * width : (head + 1) * width
            ]
        return 0

    lax.fori_loop(0, spans, place_grads, 0)
    grad_keys[...] = jnp.zeros_like(grad_keys)
    grad_values[...] = jnp.zeros_like(grad_values)

    def one_tile(tile, _):
        query = queries[tile]
        grad_out = grad_outs[tile]
        product = jnp.transpose(grad_out.astype(WIDE) * outs[tile])
        delta[...] = jnp.broadcast_to(jnp.sum(product, axis=0, keepdims=True), delta.shape)
        grad_turned[...] = jnp.zeros_like(grad_turned)

        def pair(step, masked):
            at = pl.multiple_of(step * TILE, TILE)
            key = keys[pl.ds(at, TILE), :]
            value = values[pl.ds(at, TILE), :][:, :width]
            scores = dot(key, query, ((1,), (1,)))
            probs = jnp.exp(scores - totals[tile, 0:1, :])
            if masked:
                probs = jnp.where(allowed, probs, 0.0)
            grad_probs = dot(value, grad_out, ((1,), (1,)))
            grad_scores = (probs * (grad_probs - delta[0:1, :])).astype(LOW)
            grad_values[pl.ds(at, TILE), :] += dot(probs.astype(LOW), grad_out)
            grad_keys[pl.ds(at, TILE), :] += dot(grad_scores, query)
            grad_turned[...] += dot(key, grad_scores, ((0,), (0,)))

        def before(step, _):
            pair(step, False)
            return 0

        pair(tile, True)
        lax.fori_loop(0, tile, before, 0)
        grad_queries[tile] = jnp.transpose(grad_turned[...]) * scale
        return 0

    lax.fori_loop(0, tiles, one_tile, 0)

    def finish(place, sums):
        slot = pl.multiple_of(order[place] * span, span)
        at = pl.multiple_of(place * span, span)
        part = raw[pl.ds(slot, span), :]
        cos_part = cosine[pl.ds(at, span), :]
        sin_part = sine[pl.ds(at, span), :]
        query_sum, key_sum = sums
        pieces = []
        for head in range(heads + 1):
            if head < heads:
                row = pl.multiple_of(head * TILE + (place % per_tile) * span, span)
                turned = grad_queries[place // per_tile, pl.ds(row, span), :]
                gain = query_gain[...]
            else:
                turned = grad_keys[pl.ds(at, span), :]
                gain = key_gain[...]
            normed, inverse = rms_parts(part[:, head * width : (head + 1) * width])
            back = turned * cos_part - swap_halves(turned) * sin_part
            added = jnp.sum(back * normed, axis=0, keepdims=True)
            if head < heads:
                query_sum = query_sum + added
            else:
                key_sum = key_sum + added
            pieces.append(norm_back(back, normed, inverse, gain))
        pieces.append(grad_values[pl.ds(at, span), :])
        grad_raw[pl.ds(slot, span), :] = jnp.concatenate(pieces, axis=-1).astype(LOW)
        return (query_sum, key_sum)

    start = jnp.zeros((1, width), WIDE)
    query_sum, key_sum = lax.fori_loop(0, spans, finish, (start, start))
    gain_sums[0:1, :] = query_sum
    gain_sums[1:2, :] = key_sum


def attention_backward(
    order, raw, grad_att, saved, query_gain, key_gain, cosine, sine, heads, width, span
):
    length = raw.shape[0]
    tiles = length // TILE
    vmem = pl.BlockSpec(memory_space=pltpu.VMEM)
    return pl.pallas_call(
        functools.partial(backward_body, heads=heads, width=width, span=span, length=length),
        name="attention_backward",
        in_specs=[pl.BlockSpec(memory_space=pltpu.SMEM)] + [vmem] * 11,
        out_specs=[vmem] * 2,
        out_shape=[
            jax.ShapeDtypeStruct(raw.shape, LOW),
            jax.ShapeDtypeStruct((2, width), WIDE),
        ],
        scratch_shapes=[
            pltpu.VMEM((tiles, heads * TILE, width), LOW),
            pltpu.VMEM((tiles, heads * TILE, width), WIDE),
            pltpu.VMEM((length, width), WIDE),
            pltpu.VMEM((length, width), WIDE),
            pltpu.VMEM((width, heads * TILE), WIDE),
            pltpu.VMEM((8, heads * TILE), WIDE),
        ],
        compiler_params=pltpu.CompilerParams(vmem_limit_bytes=48 * 1024 * 1024),
    )(order, raw, grad_att, *saved, query_gain, key_gain, cosine, sine)


def exchange(value, size, offset):
    return lax.ppermute(value, "seq", [(index, index ^ offset) for index in range(size)])


def block_order(size):
    return list(range(0, size, 2)) + list(range(1, size, 2))


def gather_rows(block, size):
    evens = [block] + [exchange(block, size, offset) for offset in range(2, size, 2)]
    odds = [exchange(part, size, 1) for part in evens]
    return jnp.concatenate(evens + odds, axis=0)


def scatter_rows(multiply, size, rows):
    half = size // 2
    odds = multiply(half * rows, size * rows).astype(LOW)
    arrived = exchange(odds, size, 1)
    evens = multiply(0, half * rows) + arrived.astype(WIDE)
    total = evens[:rows]
    for place in range(1, half):
        part = evens[place * rows : (place + 1) * rows].astype(LOW)
        total = total + exchange(part, size, 2 * place).astype(WIDE)
    return total


def per_device(
    n_seq, n_fsdp,
    tokens, span_ids, attn_gain, w_query, w_key, w_value, query_gain, key_gain,
    w_out, ffn_gain, w_gate, w_up, w_down, cotangent,
):
    slots, span, model = tokens.shape[1:]
    rows = slots * span
    length = rows * n_seq
    width = query_gain.shape[0]
    strip = w_query.shape[0]
    heads_all = w_query.shape[1] // width
    kv_all = w_key.shape[1] // width
    heads = heads_all // n_seq
    repeats = n_seq // kv_all
    hidden_all = w_gate.shape[1]
    hidden = hidden_all // n_seq
    me = lax.axis_index("seq")

    own_low = tokens.reshape(rows, model)
    own_cot = cotangent.reshape(rows, model)
    inputs_low = gather_rows(own_low, n_seq)

    pack = jnp.concatenate(
        [
            w_query.reshape(strip, n_seq, heads * width),
            jnp.repeat(w_key.reshape(strip, kv_all, width), repeats, axis=1),
            jnp.repeat(w_value.reshape(strip, kv_all, width), repeats, axis=1),
        ],
        axis=-1,
    ).transpose(1, 0, 2)
    pack = lax.all_to_all(pack, "seq", 0, 0, tiled=True)
    full_qkv = lax.all_gather(pack, "fsdp", axis=1).reshape(model, -1)
    full_out = lax.all_gather(w_out, "fsdp", axis=0, tiled=True)
    pack = jnp.stack(
        [w_gate.reshape(strip, n_seq, hidden), w_up.reshape(strip, n_seq, hidden)]
    ).transpose(2, 0, 1, 3)
    pack = lax.all_to_all(pack, "seq", 0, 0, tiled=True).transpose(1, 0, 2, 3)
    full_both = lax.all_gather(pack, "fsdp", axis=2).reshape(2, model, hidden)
    full_gate, full_up = full_both[0], full_both[1]
    full_down = lax.all_gather(w_down, "fsdp", axis=0, tiled=True)

    grads_low = gather_rows(own_cot, n_seq)

    owners = me ^ jnp.array(block_order(n_seq), jnp.int32)
    row_spans = span_ids.reshape(n_seq, slots)[owners].reshape(-1)
    places = jnp.arange(n_seq * slots, dtype=jnp.int32)
    order = jnp.sum(
        jnp.where(row_spans[None, :] == places[:, None], places[None, :], 0), axis=1
    ).astype(jnp.int32)
    cosine, sine = rope_tables(length, width)
    query_row = query_gain.reshape(1, width)
    key_row = key_gain.reshape(1, width)

    normed_all, _ = rms_parts(inputs_low.astype(WIDE))
    low_one = (normed_all * attn_gain).astype(LOW)
    raw = dot(low_one, full_qkv)
    attended, *saved = attention_forward(
        order, raw, query_row, key_row, cosine, sine, heads, width, span
    )
    branch = scatter_rows(lambda a, b: dot(attended[a:b], full_out), n_seq, rows)
    inputs = own_low.astype(WIDE)
    middle = inputs + branch
    normed_two, inverse_two = rms_parts(middle)
    low_two = gather_rows((normed_two * ffn_gain).astype(LOW), n_seq)

    gate = dot(low_two, full_gate)
    up_proj = dot(low_two, full_up)
    sigmoid_gate = jax.nn.sigmoid(gate)
    silu_gate = gate * sigmoid_gate
    hidden_low = (silu_gate * up_proj).astype(LOW)
    grad_hidden = dot(grads_low, full_down, ((1,), (1,)))
    grad_gate = (
        grad_hidden * up_proj * sigmoid_gate * (1.0 + gate * (1.0 - sigmoid_gate))
    ).astype(LOW)
    grad_up = (grad_hidden * silu_gate).astype(LOW)
    grad_two = scatter_rows(
        lambda a, b: dot(grad_gate[a:b], full_gate, ((1,), (1,)))
        + dot(grad_up[a:b], full_up, ((1,), (1,))),
        n_seq,
        rows,
    )
    grad_ffn_gain = jnp.sum(grad_two * normed_two, axis=0)
    grad_middle = own_cot.astype(WIDE) + norm_back(grad_two, normed_two, inverse_two, ffn_gain)
    grad_branch = gather_rows(grad_middle.astype(LOW), n_seq)
    result = middle + scatter_rows(lambda a, b: dot(hidden_low[a:b], full_down), n_seq, rows)
    outputs = result.astype(LOW).reshape(tokens.shape)

    grad_wdown = lax.psum_scatter(
        dot(hidden_low, grads_low, ((0,), (0,))).astype(LOW),
        "fsdp", scatter_dimension=0, tiled=True,
    ).astype(WIDE)
    grad_both = jnp.stack(
        [dot(low_two, grad_gate, ((0,), (0,))), dot(low_two, grad_up, ((0,), (0,)))]
    ).astype(LOW)
    grad_both = grad_both.reshape(2, n_seq, n_fsdp, strip, hidden).transpose(2, 1, 0, 3, 4)
    grad_both = lax.psum_scatter(grad_both, "fsdp", scatter_dimension=0)
    grad_both = lax.all_to_all(grad_both, "seq", 0, 0, tiled=True)
    grad_both = grad_both.transpose(1, 2, 0, 3).astype(WIDE).reshape(2, strip, hidden_all)

    grad_att = dot(grad_branch, full_out, ((1,), (1,))).astype(LOW)
    grad_wout = lax.psum_scatter(
        dot(attended, grad_branch, ((0,), (0,))).astype(LOW),
        "fsdp", scatter_dimension=0, tiled=True,
    ).astype(WIDE)
    grad_raw, head_gains = attention_backward(
        order, raw, grad_att, saved, query_row, key_row, cosine, sine, heads, width, span
    )
    grad_one = scatter_rows(lambda a, b: dot(grad_raw[a:b], full_qkv, ((1,), (1,))), n_seq, rows)
    normed_one, inverse_one = rms_parts(inputs)
    grad_attn_gain = jnp.sum(grad_one * normed_one, axis=0)
    grad_inputs = grad_middle + norm_back(grad_one, normed_one, inverse_one, attn_gain)

    grad_qkv = dot(low_one, grad_raw, ((0,), (0,))).astype(LOW)
    grad_qkv = grad_qkv.reshape(n_seq, n_fsdp, strip, -1).transpose(1, 0, 2, 3)
    grad_qkv = lax.psum_scatter(grad_qkv, "fsdp", scatter_dimension=0)
    grad_qkv = lax.all_to_all(grad_qkv, "seq", 0, 0, tiled=True).transpose(1, 0, 2).astype(WIDE)
    grad_wquery = grad_qkv[:, :, : heads * width].reshape(strip, heads_all * width)
    grad_wkv = grad_qkv[:, :, heads * width :].reshape(strip, kv_all, repeats, 2, width).sum(axis=2)
    grad_wkey = grad_wkv[:, :, 0].reshape(strip, kv_all * width)
    grad_wvalue = grad_wkv[:, :, 1].reshape(strip, kv_all * width)

    sums = lax.psum(
        jnp.concatenate([grad_attn_gain, grad_ffn_gain, head_gains.reshape(-1)]),
        ("seq", "fsdp"),
    )
    return (
        outputs,
        grad_inputs.reshape(tokens.shape),
        sums[:model],
        grad_wquery,
        grad_wkey,
        grad_wvalue,
        sums[2 * model : 2 * model + width],
        sums[2 * model + width :],
        grad_wout,
        sums[model : 2 * model],
        grad_both[0],
        grad_both[1],
        grad_wdown,
    )


def solution(mesh):
    whole = P()
    rows = P(("seq", "fsdp"), None)
    blocks = P("fsdp", "seq", None, None)
    return jax.shard_map(
        functools.partial(per_device, mesh.shape["seq"], mesh.shape["fsdp"]),
        mesh=mesh,
        in_specs=(
            blocks, P("fsdp", None), whole, rows, rows, rows, whole, whole,
            rows, whole, rows, rows, rows, blocks,
        ),
        out_specs=(
            blocks, blocks, whole, rows, rows, rows, whole, whole,
            rows, whole, rows, rows, rows,
        ),
        check_vma=False,
    )
```
